32 devices in a mesh: parts: 2 (over y), wide: 4 (over z), narrow: 4 (over x, core).
Axes of the slice: x: 2, y: 2, z: 4, core: 2. Of those that a mesh axis runs over, the one named last changes fastest.
Arguments:
- recording: bfloat16 [64, 512, 2048], P(('parts', 'wide'), None, 'narrow'), parts along dimension 0, may hold values from -6 to 6
- offsets: int32 [2, 64], P(None, 'parts'), parts along dimension 1, may hold values from -4 to 4
- center_rows: int32 [8, 4, 32], P(('parts', 'wide'), 'narrow'), parts along dimension 0, may hold values from 0 to 127
- center_cols: int32 [8, 4, 32], P(('parts', 'wide'), 'narrow'), parts along dimension 0, may hold values from 0 to 511
- decays: float32 [8, 4, 32], P(('parts', 'wide'), 'narrow'), parts along dimension 0, may hold values from 0.3 to 0.95
Outputs:
- footprints: bfloat16 [8, 4, 32, 135168], P(('parts', 'wide'), 'narrow'), parts along dimension 0
- traces: float32 [8, 4, 32, 16], P(('parts', 'wide'), 'narrow'), parts along dimension 0
- spikes: float32 [8, 4, 32, 16], P(('parts', 'wide'), 'narrow'), parts along dimension 0
The draws below stay inside these ranges and needn't reach their ends.
There are 2 independent parts, one for each index of `parts`. The reference program is written for one: setup_inputs(seed, part) draws one part's arguments, and reference() takes and returns one part's arrays. A program takes and returns all parts, laid end to end along the dimension named above; each array names one. Nothing has to cross between parts.
All inputs are finite; a program needn't handle non-finite values.
Results may differ from the reference program's by a relative error of at most 0.013.
The reference program's roundings to bfloat16 on the way (of `registered`, `observed` and `residual`) count: a program that leaves them out, or rounds other values in their place, can miss the bound.
Values may be sent and summed in bfloat16 or wider, within the bound.
No kernel may reach another device: no remote copies, remote signals or barrier semaphores. Data moves between devices by JAX's collectives and lax.ppermute only.
A program may use at most 128 MiB of HBM per device.

```python
import math
import jax
import jax.numpy as jnp
from jax import lax

W = 2048
H = 512
PLANES = 2
VOLUMES = 16
K = 32
MARGIN = 8
SHIFT_MAX = 4
RADIUS = 12
ITERS = 3
FRAMES = 32
PATCH_ROWS = 4
PATCH_COLS = 4
ROWS_PATCH = 128
COLS_PATCH = 512


def place_ends(array, rng, least, largest):
    extent = array.shape
    place = [jax.random.randint(jax.random.fold_in(rng, axis), (), 0, extent[axis]) for axis in range(len(extent))]
    array = array.at[tuple(place)].set(least)
    longest = extent.index(max(extent))
    place[longest] = (place[longest] + 1) % extent[longest]
    return array.at[tuple(place)].set(largest)


def block_scale(own_key, extent, cuts, low, top_value):
    factor_of, own = 1.0, jax.random.fold_in(own_key, 6)
    for axis_at, shards_of in cuts:
        heights = jnp.exp(jax.random.uniform(jax.random.fold_in(own, axis_at), (shards_of,), jnp.float32, low / len(cuts), top_value / len(cuts)))
        factor_of = factor_of * jnp.repeat(heights, extent[axis_at] // shards_of).reshape([-1 if axis == axis_at else 1 for axis in range(len(extent))])
    return factor_of


def bell_draw(key, shape, scale, bound, cuts=(), held_as=jnp.bfloat16):
    gain = block_scale(key, shape, cuts, -0.22, 0.18) if cuts else 1.0
    values = jax.random.normal(key, shape, jnp.float32) * scale * gain
    return jnp.minimum(jnp.maximum(values, -bound), bound).astype(held_as)


def setup_inputs(seed: int = 0, part: int = 0) -> dict:
    streams_of = jax.random.split(jax.random.key(seed), 6)
    part_keys = jax.random.split(jax.random.fold_in(streams_of[5], part), 6)
    recording = bell_draw(part_keys[0], (FRAMES, H, W), 1.0, 6.0, ((0, 4), (2, 4)))
    offsets = place_ends(jax.random.randint(part_keys[1], (2, FRAMES), 0 - SHIFT_MAX, SHIFT_MAX + 1), jax.random.fold_in(part_keys[1], 1), 0 - SHIFT_MAX, SHIFT_MAX).astype(jnp.int32)
    center_rows = place_ends(jax.random.randint(part_keys[2], (PATCH_ROWS, PATCH_COLS, K), 0, ROWS_PATCH), jax.random.fold_in(part_keys[2], 1), 0, ROWS_PATCH - 1).astype(jnp.int32)
    center_cols = place_ends(jax.random.randint(part_keys[3], (PATCH_ROWS, PATCH_COLS, K), 0, COLS_PATCH), jax.random.fold_in(part_keys[3], 1), 0, COLS_PATCH - 1).astype(jnp.int32)
    decays = jnp.clip(jnp.exp(math.log(0.95) - 1.1526795 * jax.random.uniform(part_keys[4], (PATCH_ROWS, PATCH_COLS, K), jnp.float32) ** block_scale(part_keys[4], (PATCH_ROWS, PATCH_COLS, K), ((0, 4), (1, 4)), -0.2, 0.2)), 0.3, 0.95)
    return dict(recording=recording, offsets=offsets, center_rows=center_rows, center_cols=center_cols, decays=decays)


RIDGE = 1.0


def narrowed(values):
    return lax.optimization_barrier(values.astype(jnp.bfloat16)).astype(jnp.float32)


def initial_state(rows_center, cols_center, column_index, rows_patch, cols_patch, width_total):
    ext_width = cols_patch + 2 * MARGIN
    row_pos = jnp.arange(rows_patch, dtype=jnp.int32).astype(jnp.float32)
    col_pos = jnp.arange(ext_width, dtype=jnp.int32) - MARGIN
    global_col = column_index * cols_patch + col_pos
    inside = ((global_col >= 0) & (global_col < width_total)).astype(jnp.float32)
    row_bump = jnp.maximum(0.0, 1.0 - jnp.abs(row_pos[None, :] - rows_center[:, None].astype(jnp.float32)) / RADIUS)
    col_bump = jnp.maximum(0.0, 1.0 - jnp.abs(col_pos.astype(jnp.float32)[None, :] - cols_center[:, None].astype(jnp.float32)) / RADIUS)
    col_bump = col_bump * inside[None, :]
    planar = row_bump[:, :, None] * col_bump[:, None, :]
    initial = jnp.broadcast_to(planar[:, None], (rows_center.shape[0], PLANES, rows_patch, ext_width)).reshape(rows_center.shape[0], -1)
    support = jnp.broadcast_to(inside, (PLANES, rows_patch, ext_width)).reshape(-1)
    return initial, support


def reference(recording, offsets, center_rows, center_cols, decays):
    frames_all, height, width_total = recording.shape
    registered = lax.map(lambda record: jnp.roll(record[0], (record[1], record[2]), (0, 1)), (recording, offsets[0], offsets[1]))
    template = jnp.sum(registered.reshape(PLANES, VOLUMES, height, width_total), axis=1, dtype=jnp.float32) / VOLUMES
    rows_patch = height // PATCH_ROWS
    cols_patch = width_total // PATCH_COLS
    ext_width = cols_patch + 2 * MARGIN

    def one_row(row_index):
        picked = lax.dynamic_slice_in_dim(registered, row_index * rows_patch, rows_patch, 1)
        baseline = lax.dynamic_slice_in_dim(template, row_index * rows_patch, rows_patch, 1)
        observed = (picked.reshape(PLANES, VOLUMES, rows_patch, width_total).astype(jnp.float32) - baseline[:, None]).transpose(1, 0, 2, 3)
        observed = narrowed(observed)
        rows_center = lax.dynamic_index_in_dim(center_rows, row_index, 0, keepdims=False)
        cols_center = lax.dynamic_index_in_dim(center_cols, row_index, 0, keepdims=False)
        decay_row = lax.dynamic_index_in_dim(decays, row_index, 0, keepdims=False)
        pairs = [initial_state(rows_center[column], cols_center[column], column, rows_patch, cols_patch, width_total) for column in range(PATCH_COLS)]
        footprints = jnp.stack([pair[0] for pair in pairs])
        support = jnp.stack([pair[1] for pair in pairs])
        traces = jnp.zeros((PATCH_COLS, K, VOLUMES), jnp.float32)

        def residual_ext(footprints, traces):
            model_ext = jnp.einsum('ckv,cke->cve', narrowed(traces), narrowed(footprints), precision=lax.Precision.HIGHEST)
            model_ext = model_ext.reshape(PATCH_COLS, VOLUMES, PLANES, rows_patch, ext_width)
            canvas = jnp.zeros((VOLUMES, PLANES, rows_patch, width_total + 2 * MARGIN), jnp.float32)
            for column in range(PATCH_COLS):
                canvas = canvas.at[..., column * cols_patch:column * cols_patch + ext_width].add(model_ext[column])
            model_core = canvas[..., MARGIN:MARGIN + width_total]
            residual = narrowed(observed - model_core)
            padded = jnp.pad(residual, ((0, 0), (0, 0), (0, 0), (MARGIN, MARGIN)))
            pieces = [padded[..., column * cols_patch:column * cols_patch + ext_width] for column in range(PATCH_COLS)]
            return jnp.stack(pieces).reshape(PATCH_COLS, VOLUMES, -1)

        for sweep in range(ITERS):
            residual = residual_ext(footprints, traces)
            project = jnp.einsum('cke,cve->ckv', narrowed(footprints), residual, precision=lax.Precision.HIGHEST)
            traces = jnp.maximum(0.0, traces + project / (jnp.sum(footprints * footprints, axis=-1) + RIDGE)[..., None])
            residual = residual_ext(footprints, traces)
            update = jnp.einsum('ckv,cve->cke', narrowed(traces), residual, precision=lax.Precision.HIGHEST)
            footprints = jnp.maximum(0.0, footprints + support[:, None, :] * update / (jnp.sum(traces * traces, axis=-1) + RIDGE)[..., None])
        previous = jnp.concatenate([jnp.zeros((PATCH_COLS, K, 1), jnp.float32), traces[..., :-1]], axis=-1)
        spikes = jnp.maximum(0.0, traces - decay_row[..., None] * previous)
        return footprints.astype(jnp.bfloat16), traces, spikes

    return lax.map(one_row, jnp.arange(PATCH_ROWS, dtype=jnp.int32))
```

```python
import functools

import jax
import jax.numpy as jnp
from jax import lax
from jax.experimental import pallas as pl
from jax.experimental.pallas import tpu as pltpu
from jax.sharding import PartitionSpec as P

PLANES = 2
VOLUMES = 16
MARGIN = 8
SHIFT_MAX = 4
RADIUS = 12
ITERS = 3
RIDGE = 1.0
LANES = 128
EDGE = 16
GROUP = 8


SMEM = pl.BlockSpec(memory_space=pltpu.SMEM)
VMEM = pl.BlockSpec(memory_space=pltpu.VMEM)
f32, bf16 = jnp.float32, jnp.bfloat16


def lane_iota(rows=1):
    return lax.broadcasted_iota(jnp.int32, (rows, LANES), 1)


def nt_dot(a, b):
    return lax.dot_general(a, b, (((1,), (1,)), ((), ())), preferred_element_type=f32)


def rows_kernel(plan, wide, rows_patch, chunk_rows, index_ref, offsets_ref, frame_ref, *refs):
    frames, height, cols = pl.num_programs(0), frame_ref.shape[1], frame_ref.shape[2]
    wide_at, frame = index_ref[0], pl.program_id(0)
    scratch = refs[-1]
    blocks, edges = refs[: len(plan) * wide], refs[len(plan) * wide : -1]
    values = frame_ref[0].astype(f32)
    scratch[pl.ds(GROUP, height), :] = values
    scratch[pl.ds(0, GROUP), :] = values[height - GROUP :]
    scratch[pl.ds(height + GROUP, GROUP), :] = values[:GROUP]
    move = offsets_ref[0, wide_at * frames + frame]
    back = lax.rem(2 * GROUP - move, GROUP)
    floor = GROUP - move - back
    turn = lax.rem(GROUP - back, GROUP)
    stays = lax.broadcasted_iota(jnp.int32, (GROUP, cols), 0) < GROUP - back
    mine = lane_iota(chunk_rows) // EDGE == frame
    for step in range(wide):
        target = lax.rem(wide_at + step, wide)
        for place, chunk in enumerate(plan):
            start = target * rows_patch + chunk * chunk_rows + floor
            window = scratch[pl.ds(pl.multiple_of(start, GROUP), chunk_rows + GROUP), :]
            turned = [pltpu.roll(window[at : at + GROUP], turn, 0) for at in range(0, chunk_rows + GROUP, GROUP)]
            rolled = jnp.concatenate(
                [jnp.where(stays, turned[at], turned[at + 1]) for at in range(chunk_rows // GROUP)], axis=0
            )
            blocks[place * wide + step][0] = rolled.astype(bf16)
            part = pl.ds(place * chunk_rows, chunk_rows)
            tail = pltpu.roll(rolled[:, cols - LANES :], lax.rem(frame * EDGE + EDGE, LANES), 1)
            head = pltpu.roll(rolled[:, :LANES], frame * EDGE, 1)
            for ref, value in ((edges[2 * step], tail), (edges[2 * step + 1], head)):
                ref[part, :] = jnp.where(mine, value, ref[part, :].astype(f32)).astype(bf16)


def shift_rows(index, offsets, recording, plan, wide, rows_patch, chunk_rows):
    frames, height, cols = recording.shape
    block = jax.ShapeDtypeStruct((frames, chunk_rows, cols), bf16)
    edge = jax.ShapeDtypeStruct((len(plan) * chunk_rows, LANES), bf16)
    outs = pl.pallas_call(
        functools.partial(rows_kernel, plan, wide, rows_patch, chunk_rows),
        grid=(frames,),
        in_specs=[SMEM, SMEM, pl.BlockSpec((1, height, cols), lambda f: (f, 0, 0))],
        out_specs=[pl.BlockSpec((1, chunk_rows, cols), lambda f: (f, 0, 0))] * (len(plan) * wide)
        + [pl.BlockSpec(edge.shape, lambda f: (0, 0))] * (2 * wide),
        out_shape=[block] * (len(plan) * wide) + [edge] * (2 * wide),
        scratch_shapes=[pltpu.VMEM((height + 2 * GROUP, cols), f32)],
        name="shift_rows",
    )(index, offsets, recording)
    count = len(plan) * wide
    blocks = [outs[i * wide : (i + 1) * wide] for i in range(len(plan))]
    return blocks, outs[count::2], outs[count + 1 :: 2]


def bump(distance):
    return jnp.maximum(0.0, 1.0 - jnp.abs(distance) * (1.0 / RADIUS))


def initial_kernel(cols, narrow, index_ref, centers_ref, core_ref, strip_ref, left_ref, right_ref, total_ref):
    group = pl.program_id(0)
    tiles = cols // LANES
    narrow_at = index_ref[1]
    ext = cols + 2 * MARGIN
    lane = lane_iota()
    first = (group * GROUP).astype(f32)
    own_row, own_col = centers_ref[:, 0:1], centers_ref[:, 1:2]
    least = jnp.where(narrow_at == 0, MARGIN, 0)
    most = jnp.where(narrow_at == narrow - 1, cols + MARGIN, ext)
    total = jnp.zeros((core_ref.shape[0], LANES), f32)
    for tile in range(GROUP * tiles + 1):
        q, u = tile // tiles, tile % tiles
        col = LANES * u + lane - EDGE * q
        row = jnp.full_like(lane, q)
        if u == 0:
            earlier = lane < EDGE * q
            col = jnp.where(earlier, col + ext, col)
            row = jnp.where(earlier, q - 1, q)
        inside = ((col >= least) & (col < most) & (row < GROUP)).astype(f32)
        row_bump = bump(first + row.astype(f32) - own_row)
        col_bump = bump((col - MARGIN).astype(f32) - own_col) * inside
        planar = row_bump * col_bump
        total += planar * planar
        if u == 0:
            strip_ref[:, pl.ds(q * LANES, LANES)] = planar.astype(bf16)
        else:
            core_ref[:, pl.ds((q * (tiles - 1) + u - 1) * LANES, LANES)] = planar.astype(bf16)
    row = first + (lane // EDGE).astype(f32)
    col = (lane % EDGE - MARGIN).astype(f32)
    left = bump(row - centers_ref[:, 2:3]) * bump(col + cols - centers_ref[:, 3:4])
    right = bump(row - centers_ref[:, 4:5]) * bump(col - centers_ref[:, 5:6])
    left_ref[...] = jnp.where(narrow_at > 0, left, 0.0).astype(bf16)
    right_ref[...] = jnp.where(narrow_at < narrow - 1, right, 0.0).astype(bf16)

    @pl.when(group == 0)
    def _():
        total_ref[...] = jnp.zeros_like(total_ref)

    total_ref[...] += jnp.broadcast_to(jnp.sum(total, axis=1, keepdims=True) * PLANES, total_ref.shape)


def initial_footprints(index, centers, rows_patch, cols, narrow):
    comps = centers.shape[0]
    groups = rows_patch // GROUP
    core = GROUP * (cols - LANES)
    strip = (GROUP + 1) * LANES
    widths = (core, strip, LANES, LANES)
    return pl.pallas_call(
        functools.partial(initial_kernel, cols, narrow),
        grid=(groups,),
        in_specs=[SMEM, VMEM],
        out_specs=[pl.BlockSpec((comps, width), lambda g: (g, 0)) for width in widths]
        + [pl.BlockSpec((comps, LANES), lambda g: (0, 0))],
        out_shape=[jax.ShapeDtypeStruct((groups * comps, width), bf16) for width in widths]
        + [jax.ShapeDtypeStruct((comps, LANES), f32)],
        name="initial",
    )(index, centers)


def observe_kernel(wide, narrow, first, last, index_ref, offsets_ref, *refs):
    frames_refs, refs = refs[:wide], refs[wide:]
    from_left, from_right, refs = refs[:wide], refs[wide : 2 * wide], refs[2 * wide :]
    core0_ref, strip0_ref, total_ref, *_ = refs
    core_ref, strip_ref, out_ref, scratch = refs[-4:]
    frames, rows, cols = frames_refs[0].shape
    tiles = cols // LANES
    comps = core0_ref.shape[0] // (rows // GROUP)
    wide_at, narrow_at = index_ref[0], index_ref[1]
    lane = lane_iota(rows)
    for step in range(wide):
        source = lax.rem(wide_at + wide - step, wide)
        left, right = from_left[step][...].astype(f32), from_right[step][...].astype(f32)
        for i in range(frames):
            frame = source * frames + i
            move = offsets_ref[1, frame] + MARGIN
            after = lane >= move
            block = frames_refs[step][i].astype(f32)
            before = pltpu.roll(left, lax.rem(move + (2 * LANES - EDGE - EDGE * i), LANES), 1)
            for tile in range(tiles + 1):
                if tile < tiles:
                    rolled = pltpu.roll(block[:, tile * LANES : (tile + 1) * LANES], move, 1)
                else:
                    rolled = pltpu.roll(right, lax.rem(move + (LANES - EDGE * i), LANES), 1)
                scratch[tile, pl.ds(pl.multiple_of(frame * rows, rows), rows), :] = jnp.where(after, rolled, before)
                before = rolled
    lane = lane_iota(VOLUMES)
    drop_left = (lane < MARGIN) & (narrow_at == 0)
    drop_right = (lane >= MARGIN) & (narrow_at == narrow - 1)
    for plane in range(PLANES):
        for half in range(rows // GROUP):
            out_rows = pl.ds(half * VOLUMES, VOLUMES)
            pending = None
            for j in range(GROUP):
                turned = []
                for tile in range(tiles + 1):
                    at = plane * VOLUMES * rows + half * GROUP + j
                    value = scratch[tile, pl.ds(at, VOLUMES, stride=rows), :]
                    value = value - jnp.sum(value, axis=0, keepdims=True) * (1.0 / VOLUMES)
                    if tile == 0:
                        value = jnp.where(drop_left, 0.0, value)
                    if tile == tiles:
                        value = jnp.where(drop_right, 0.0, value)
                    turned.append(pltpu.roll(value, j * EDGE, 1) if j else value)
                merged = turned[0] if pending is None else jnp.where(lane < EDGE * j, pending, turned[0])
                strip_ref[plane, out_rows, j * LANES : (j + 1) * LANES] = merged.astype(bf16)
                for tile in range(1, tiles):
                    merged = jnp.where(lane < EDGE * j, turned[tile - 1], turned[tile]) if j else turned[tile]
                    at = (j * (tiles - 1) + tile - 1) * LANES
                    core_ref[plane, out_rows, at : at + LANES] = merged.astype(bf16)
                pending = jnp.where(lane < EDGE * j, turned[tiles - 1], turned[tiles]) if j else turned[tiles]
            end = jnp.where(lane < EDGE * GROUP, pending, 0.0)
            strip_ref[plane, out_rows, GROUP * LANES : (GROUP + 1) * LANES] = end.astype(bf16)

    @pl.when(pl.program_id(0) == 0)
    def _():
        out_ref[...] = jnp.zeros_like(out_ref) if first else refs[3][...]

    acc = jnp.zeros((comps, PLANES * VOLUMES), f32)
    for half in range(rows // GROUP):
        of_comps, of_rows = pl.ds(half * comps, comps), pl.ds(half * VOLUMES, VOLUMES)
        for begin, seen in ((core0_ref, core_ref), (strip0_ref, strip_ref)):
            both = jnp.concatenate([seen[plane, of_rows, :] for plane in range(PLANES)], axis=0)
            acc += nt_dot(begin[of_comps, :], both)
    summed = acc[:, :VOLUMES] + acc[:, VOLUMES:]
    out_ref[:, :VOLUMES] += summed
    if last:

        @pl.when(pl.program_id(0) == pl.num_programs(0) - 1)
        def _():
            out_ref[...] = jnp.maximum(0.0, out_ref[...] / (total_ref[...] + RIDGE))


def observe(index, offsets, blocks, lefts, rights, edge_at, row_at, begin, state, shapes, narrow, last):
    wide = len(blocks)
    frames, rows, cols = blocks[0].shape
    step_rows = 2 * GROUP
    core0, strip0, total = begin
    partial_shape, core_shape, strip_shape = shapes
    tiles = cols // LANES
    halves = step_rows // GROUP
    comps = total.shape[0]
    at, edge = row_at // step_rows, edge_at // step_rows
    frame_spec = pl.BlockSpec((frames, step_rows, cols), lambda i: (0, i, 0))
    edge_spec = pl.BlockSpec((step_rows, LANES), lambda i: (edge + i, 0))
    fixed = pl.BlockSpec((comps, LANES), lambda i: (0, 0))
    wide_of = (core_shape.shape[2], strip_shape.shape[2])
    first_specs = [pl.BlockSpec((halves * comps, width), lambda i: (at + i, 0)) for width in wide_of]
    seen_specs = [pl.BlockSpec((PLANES, halves * VOLUMES, width), lambda i: (0, at + i, 0)) for width in wide_of]
    args = [index, offsets, *blocks, *lefts, *rights, core0, strip0, total, *state]
    return pl.pallas_call(
        functools.partial(observe_kernel, wide, narrow, not state, last),
        grid=(rows // step_rows,),
        in_specs=[SMEM, SMEM]
        + [frame_spec] * wide
        + [edge_spec] * (2 * wide)
        + first_specs
        + [fixed]
        + ([fixed] + [pl.BlockSpec(memory_space=pl.ANY)] * 2 if state else []),
        out_specs=seen_specs + [fixed],
        out_shape=[core_shape, strip_shape, partial_shape],
        input_output_aliases={len(args) - 2: 0, len(args) - 1: 1} if state else {},
        scratch_shapes=[pltpu.VMEM((tiles + 1, wide * frames * step_rows, LANES), f32)],
        name="observe",
    )(*args)


def spread(trace, groups, down_ref, across_ref):
    comps = trace.shape[0]
    stacked = jnp.concatenate([trace.astype(bf16)] * groups, axis=0)
    shape = (groups * VOLUMES, LANES)
    pick = lax.broadcasted_iota(jnp.int32, shape, 0) % VOLUMES == lax.broadcasted_iota(jnp.int32, shape, 1)
    pick = pick.astype(f32).astype(bf16)
    for ref, first, second, row_unit, col_unit in (
        (down_ref, pick, stacked, VOLUMES, comps),
        (across_ref, stacked, pick, comps, VOLUMES),
    ):
        full = nt_dot(first, second)
        same = (
            lax.broadcasted_iota(jnp.int32, full.shape, 0) // row_unit
            == lax.broadcasted_iota(jnp.int32, full.shape, 1) // col_unit
        )
        ref[...] = jnp.where(same, full, 0.0).astype(bf16)


def inverse_norm(trace, groups):
    norm = 1.0 / (jnp.sum(trace * trace, axis=1, keepdims=True) + RIDGE)
    return jnp.concatenate([norm] * groups, axis=0)


def folded(full, groups, comps):
    same = (
        lax.broadcasted_iota(jnp.int32, full.shape, 0) // comps
        == lax.broadcasted_iota(jnp.int32, full.shape, 1) // VOLUMES
    )
    kept = jnp.where(same, full, 0.0)
    rows = sum(kept[g * comps : (g + 1) * comps] for g in range(groups))
    return sum(rows[:, g * VOLUMES : (g + 1) * VOLUMES] for g in range(groups))


def core_kernel(groups, last, trace_ref, seen_ref, prints_ref, *refs):
    if last:
        out_ref, down, across, norm = refs
    else:
        out_ref, project_ref, square_ref, down, across, norm, acc, squares = refs
    at = pl.program_id(0)
    comps = trace_ref.shape[0]

    @pl.when(at == 0)
    def _():
        trace = trace_ref[...]
        spread(trace, groups, down, across)
        norm[...] = jnp.broadcast_to(inverse_norm(trace, groups), norm.shape)
        if not last:
            acc[...] = jnp.zeros_like(acc)
            squares[...] = jnp.zeros_like(squares)

    width = 2 * LANES

    def body(i, carry):
        part = pl.ds(pl.multiple_of(i * width, width), width)
        prints, seen = prints_ref[:, part], seen_ref[:, part].astype(f32)
        model = jnp.dot(down[...], prints, preferred_element_type=f32)
        residual = (seen - model).astype(bf16)
        update = jnp.dot(across[...], residual, preferred_element_type=f32)
        scale = jnp.concatenate([norm[...]] * 2, axis=1)
        new = jnp.maximum(0.0, prints.astype(f32) + update * scale)
        low = new.astype(bf16)
        out_ref[:, part] = low
        if not last:
            squared = new * new
            squares[...] += squared[:, :LANES] + squared[:, LANES:]
            model = jnp.dot(down[...], low, preferred_element_type=f32)
            residual = (seen - model).astype(bf16)
            acc[...] += nt_dot(low, residual)
        return carry

    lax.fori_loop(0, prints_ref.shape[1] // width, body, 0, unroll=4)
    if not last:

        @pl.when(at == pl.num_programs(0) - 1)
        def _():
            project_ref[...] = jnp.zeros_like(project_ref)
            project_ref[:, :VOLUMES] = folded(acc[...], groups, comps)
            rows = sum(squares[pl.ds(g * comps, comps), :] for g in range(groups))
            square_ref[...] = jnp.broadcast_to(jnp.sum(rows, axis=1, keepdims=True), square_ref.shape)


def core_update(trace, seen, prints, groups, last):
    comps = trace.shape[0]
    count = seen.shape[0] // (groups * VOLUMES)
    held = prints.shape[0] // (groups * comps)
    width = seen.shape[1]
    block = (groups * comps, width)
    whole = jax.ShapeDtypeStruct((count * groups * comps, width), bf16)
    small = jax.ShapeDtypeStruct((comps, LANES), f32)
    fixed = pl.BlockSpec((comps, LANES), lambda b: (0, 0))
    scratch = [
        pltpu.VMEM((groups * VOLUMES, groups * comps), bf16),
        pltpu.VMEM((groups * comps, groups * VOLUMES), bf16),
        pltpu.VMEM((groups * comps, LANES), f32),
    ]
    if not last:
        scratch += [pltpu.VMEM((groups * comps, groups * VOLUMES), f32), pltpu.VMEM((groups * comps, LANES), f32)]
    return pl.pallas_call(
        functools.partial(core_kernel, groups, last),
        grid=(count,),
        in_specs=[
            fixed,
            pl.BlockSpec((groups * VOLUMES, width), lambda b: (b, 0)),
            pl.BlockSpec(block, lambda b: (lax.rem(b, held), 0)),
        ],
        out_specs=[pl.BlockSpec(block, lambda b: (b, 0))] + ([] if last else [fixed, fixed]),
        out_shape=[whole] + ([] if last else [small, small]),
        scratch_shapes=scratch,
        name="core_last" if last else "core",
    )(trace, seen, prints)


def strip_kernel(groups, tiles, narrow, last, index_ref, *refs):
    trace_refs, refs = refs[:3], refs[3:]
    seen_ref, prints_ref, left_ref, right_ref, refs = refs[0], refs[1], refs[2], refs[3], refs[4:]
    if last:
        core_ref, out_ref, refs = refs[0], refs[1], refs[2:]
    else:
        project_ref, square_ref, decays_ref, refs = refs[0], refs[1], refs[2], refs[3:]
        out_ref, left_out, right_out, trace_out, spikes_out, refs = refs[0], refs[1], refs[2], refs[3], refs[4], refs[5:]
    downs, acrosses, norms, refs = refs[:3], refs[3:6], refs[6:9], refs[9:]
    if not last:
        acc, squares = refs
    at = pl.program_id(0)
    comps = trace_refs[0].shape[0]
    narrow_at = index_ref[1]

    @pl.when(at == 0)
    def _():
        for trace_ref, down, across, norm in zip(trace_refs, downs, acrosses, norms):
            trace = trace_ref[...]
            spread(trace, groups, down, across)
            norm[...] = jnp.broadcast_to(inverse_norm(trace, groups), norm.shape)
        if not last:
            acc[...] = jnp.zeros_like(acc)
            squares[...] = jnp.zeros_like(squares)

    lane = lane_iota()
    piece, within = lane // EDGE, lane % EDGE

    def model_of(tile, prints, from_left, from_right):
        model = jnp.dot(downs[0][...], prints, preferred_element_type=f32)
        side = jnp.where(piece == tile, from_left, jnp.where(piece == tile - 1, from_right, 0.0))
        return model + side

    left, right = left_ref[...], right_ref[...]
    from_left = jnp.dot(downs[1][...], left, preferred_element_type=f32)
    from_right = jnp.dot(downs[2][...], right, preferred_element_type=f32)
    zero = jnp.zeros((groups * VOLUMES, LANES), f32)
    at_left, at_right = zero, zero
    news = []
    for tile in range(GROUP + 1):
        part = pl.ds(tile * LANES, LANES)
        prints, seen = prints_ref[:, part], seen_ref[:, part].astype(f32)
        residual = (seen - model_of(tile, prints, from_left, from_right)).astype(bf16)
        wide_residual = residual.astype(f32)
        outside = ((narrow_at == 0) & (piece == tile) & (within < MARGIN)) | (
            (narrow_at == narrow - 1) & (piece == tile - 1) & (within >= MARGIN)
        )
        supported = jnp.where(outside, 0.0, wide_residual)
        update = jnp.dot(acrosses[0][...], supported.astype(bf16), preferred_element_type=f32)
        new = jnp.maximum(0.0, prints.astype(f32) + update * norms[0][...])
        low = new.astype(bf16)
        if last:
            for g in range(groups):
                where = (g * (GROUP * tiles + 1) + tile * tiles) * LANES
                out_ref[:, where : where + LANES] = low[g * comps : (g + 1) * comps]
        else:
            out_ref[:, part] = low
            squares[...] += new * new
            at_left = jnp.where(piece == tile, wide_residual, at_left)
            at_right = jnp.where(piece == tile - 1, wide_residual, at_right)
    if last:
        size = (tiles - 1) * LANES
        for g in range(groups):
            for j in range(GROUP):
                where = (g * (GROUP * tiles + 1) + j * tiles + 1) * LANES
                out_ref[:, where : where + size] = core_ref[pl.ds(g * comps, comps), j * size : (j + 1) * size]
        return
    sides = []
    for k, side, held, ref in ((1, at_left, left, left_out), (2, at_right, right, right_out)):
        update = jnp.dot(acrosses[k][...], side.astype(bf16), preferred_element_type=f32)
        low = jnp.maximum(0.0, held.astype(f32) + update * norms[k][...]).astype(bf16)
        ref[...] = low
        sides.append(jnp.dot(downs[k][...], low, preferred_element_type=f32))
    for tile in range(GROUP + 1):
        part = pl.ds(tile * LANES, LANES)
        low, seen = out_ref[:, part], seen_ref[:, part].astype(f32)
        residual = (seen - model_of(tile, low, *sides)).astype(bf16)
        acc[...] += nt_dot(low, residual)

    @pl.when(at == pl.num_programs(0) - 1)
    def _():
        rows = sum(squares[pl.ds(g * comps, comps), :] for g in range(groups))
        total = jnp.sum(rows, axis=1, keepdims=True) + square_ref[...] + RIDGE
        project = folded(acc[...], groups, comps) + project_ref[:, :VOLUMES]
        trace = jnp.maximum(0.0, trace_refs[0][:, :VOLUMES] + project / total[:, :VOLUMES])
        trace_out[...] = jnp.zeros_like(trace_out)
        trace_out[:, :VOLUMES] = trace
        full = trace_out[...]
        previous = jnp.where(lane == 0, 0.0, pltpu.roll(full, 1, 1))
        spikes_out[...] = jnp.maximum(0.0, full - decays_ref[...] * previous)


def strip_update(index, traces, seen, prints, left, right, groups, tiles, narrow, rest, last):
    comps = traces[0].shape[0]
    count = seen.shape[0] // (groups * VOLUMES)
    held = prints.shape[0] // (groups * comps)
    width = seen.shape[1]
    rows = groups * comps
    fixed = pl.BlockSpec((comps, LANES), lambda b: (0, 0))
    block = lambda size: pl.BlockSpec((rows, size), lambda b: (b, 0))
    held_block = lambda size: pl.BlockSpec((rows, size), lambda b: (lax.rem(b, held), 0))
    in_specs = [SMEM] + [fixed] * 3 + [pl.BlockSpec((groups * VOLUMES, width), lambda b: (b, 0))]
    in_specs += [held_block(width), held_block(LANES), held_block(LANES)]
    scratch = [pltpu.VMEM((groups * VOLUMES, rows), bf16)] * 3
    scratch += [pltpu.VMEM((rows, groups * VOLUMES), bf16)] * 3 + [pltpu.VMEM((rows, LANES), f32)] * 3
    if last:
        flat = groups * (GROUP * tiles + 1) * LANES
        in_specs += [block(rest[0].shape[1])]
        out_specs = [pl.BlockSpec((comps, flat), lambda b: (0, b))]
        out_shape = [jax.ShapeDtypeStruct((comps, count * flat), bf16)]
    else:
        in_specs += [fixed] * 3
        out_specs = [block(width), block(LANES), block(LANES), fixed, fixed]
        small = jax.ShapeDtypeStruct((comps, LANES), f32)
        out_shape = [jax.ShapeDtypeStruct((count * rows, size), bf16) for size in (width, LANES, LANES)] + [small] * 2
        scratch += [pltpu.VMEM((rows, groups * VOLUMES), f32), pltpu.VMEM((rows, LANES), f32)]
    return pl.pallas_call(
        functools.partial(strip_kernel, groups, tiles, narrow, last),
        grid=(count,),
        in_specs=in_specs,
        out_specs=out_specs,
        out_shape=out_shape,
        scratch_shapes=scratch,
        name="strip_last" if last else "strip",
    )(index, *traces, seen, prints, left, right, *rest)


def neighbours(values, axis):
    count = lax.axis_size(axis)
    from_left = lax.ppermute(values, axis, [(i, i + 1) for i in range(count - 1)])
    from_right = lax.ppermute(values, axis, [(i + 1, i) for i in range(count - 1)])
    return from_left, from_right


def across(values, step, side, wide, narrow):
    if step == 0 and side == 0:
        return values
    pairs = [
        (w * narrow + n, (w + step) % wide * narrow + (n + side) % narrow) for w in range(wide) for n in range(narrow)
    ]
    return lax.ppermute(values, ("wide", "narrow"), pairs)


def shards(recording, offsets, center_rows, center_cols, decays):
    frames, height, cols = recording.shape
    wide, narrow = lax.axis_size("wide"), lax.axis_size("narrow")
    rows_patch = height // wide
    tiles = cols // LANES
    comps = decays.shape[-1]
    per_plane = rows_patch // GROUP
    groups = min(8, per_plane)
    chunk_rows = 2 * GROUP * max(1, rows_patch // (8 * GROUP))
    chunks = rows_patch // chunk_rows
    index = jnp.stack([lax.axis_index("wide"), lax.axis_index("narrow")]).astype(jnp.int32)

    centers = jnp.stack([center_rows[0, 0], center_cols[0, 0]], axis=1).astype(f32)
    plans = [(0,), tuple(range(1, chunks))] if chunks > 1 else [(0,)]
    sent = {}
    for plan in plans:
        blocks, tails, heads = shift_rows(index, offsets, recording, plan, wide, rows_patch, chunk_rows)
        for place, chunk in enumerate(plan):
            sent[chunk] = (blocks[place], tails, heads, place * chunk_rows)
    got, edges = {}, {}
    for chunk in range(chunks):
        blocks, tails, heads, edge_at = sent[chunk]
        if edge_at == 0:
            lefts = [across(tails[s], s, 1, wide, narrow) for s in range(wide)]
            rights = [across(heads[s], s, -1, wide, narrow) for s in range(wide)]
        got[chunk] = ([across(blocks[s], s, 0, wide, narrow) for s in range(wide)], lefts, rights, edge_at)
    centers_left, centers_right = neighbours(centers, "narrow")
    centers = jnp.concatenate([centers, centers_left, centers_right], axis=1)
    core0, strip0, left, right, total = initial_footprints(index, centers, rows_patch, cols, narrow)

    shapes = [jax.ShapeDtypeStruct((comps, LANES), f32)]
    shapes += [jax.ShapeDtypeStruct((PLANES, per_plane * VOLUMES, a.shape[1]), bf16) for a in (core0, strip0)]
    state = []
    for chunk in range(chunks):
        blocks, lefts, rights, edge_at = got[chunk]
        core, strip, partial = observe(
            index, offsets, blocks, lefts, rights, edge_at, chunk * chunk_rows,
            (core0, strip0, total), state, shapes, narrow, chunk == chunks - 1,
        )
        state = [partial, core, strip]
    trace = partial
    core = core.reshape(-1, core.shape[2])
    strip = strip.reshape(-1, strip.shape[2])
    decays_wide = jnp.broadcast_to(decays[0, 0][:, None], (comps, LANES))
    prints, edge = core0, strip0
    for sweep in range(ITERS - 1):
        sides = neighbours(trace, "narrow")
        prints, project, square = core_update(trace, core, prints, groups, False)
        edge, left, right, trace, spikes = strip_update(
            index, (trace, *sides), strip, edge, left, right, groups, tiles, narrow,
            (project, square, decays_wide), False,
        )
    sides = neighbours(trace, "narrow")
    (prints,) = core_update(trace, core, prints, groups, True)
    (footprints,) = strip_update(
        index, (trace, *sides), strip, edge, left, right, groups, tiles, narrow, (prints,), True
    )
    return (
        footprints[None, None],
        trace[None, None, :, :VOLUMES],
        spikes[None, None, :, :VOLUMES],
    )


def solution(mesh):
    in_specs = (
        P(("parts", "wide"), None, "narrow"),
        P(None, "parts"),
        P(("parts", "wide"), "narrow", None),
        P(("parts", "wide"), "narrow", None),
        P(("parts", "wide"), "narrow", None),
    )
    out_specs = (
        P(("parts", "wide"), "narrow", None, None),
        P(("parts", "wide"), "narrow", None, None),
        P(("parts", "wide"), "narrow", None, None),
    )
    return jax.shard_map(shards, mesh=mesh, in_specs=in_specs, out_specs=out_specs, check_vma=False)
```
